32 devices in a mesh: frame: 8 (over y, x, core), head: 4 (over z).
Axes of the slice: x: 2, y: 2, z: 4, core: 2. Of those that a mesh axis runs over, the one named last changes fastest.
Arguments:
- queries: bfloat16 [6144, 40, 128], P('frame', 'head')
- keys_values: bfloat16 [2, 6144, 40, 128], P(None, 'frame', 'head')
- head_kind: int32 [40], P('head'), may hold values from 0 to 1, as said below
- tile_neighbours: int32 [16, 2], P('frame'), may hold values from 0 to 15, as said below
- tile_mask: int32 [16, 2], P('frame'), may hold values 0 or 1
- out_weight: bfloat16 [5120, 5120], P('head'), may hold values from -0.078125 to 0.078125
Outputs:
- projected: bfloat16 [6144, 5120], P(('frame', 'head'))
The draws below stay inside these ranges and needn't reach their ends.
Inputs may be any that keep to these rules, and one draw needn't show every extreme that they name: `head_kind`: each aligned block of 10 heads holds at most 4 temporal heads, and some block holds exactly 4. `tile_neighbours`: row g names 2 distinct tiles other than g, each in the partition of g (partition g // 2), among the last 1 tiles of the partition before it, or among the first 1 tiles of the partition after it.
All inputs are finite; a program needn't handle non-finite values. No bound on the sum of `tile_mask` on one device may be relied on, other than what follows from the above.
Results may differ from the reference program's by a relative error of at most 0.015.
Values may be sent and summed in bfloat16 or wider, within the bound.
No kernel may reach another device: no remote copies, remote signals or barrier semaphores. Data moves between devices by JAX's collectives and lax.ppermute only.
A program may use at most 128 MiB of HBM per device.

```python
import jax
import jax.numpy as jnp
from jax import lax

D = 5120
HEADS = 40
HD = 128
TILE = 384
NBR = 2
FACE = 1
TILES_DEV = 2
TOK_DEV = 768
TILES = 16
TOKENS = 6144
HEADS_DEV = 10
TMAX = 4


def attention_rows(key):
    base_key = jax.random.fold_in(key, 11)
    query_draw = jax.random.normal(jax.random.fold_in(base_key, 1), (TOKENS, HEADS, HD), jnp.float32)
    key_draw = jax.random.normal(jax.random.fold_in(base_key, 2), (TOKENS, HEADS, HD), jnp.float32)
    value_draw = jax.random.normal(jax.random.fold_in(base_key, 5), (TOKENS, HEADS, HD), jnp.float32)
    return (query_draw, jnp.stack([key_draw, value_draw], axis=0))


def draw_queries(key, part):
    return attention_rows(key)[0].astype(jnp.bfloat16)


def draw_keys_values(key, part):
    return attention_rows(key)[1].astype(jnp.bfloat16)


def draw_head_kind(key, part):
    block_count = HEADS // HEADS_DEV
    counts = jax.random.randint(jax.random.fold_in(key, 21), (block_count,), 0, TMAX + 1)
    forced = jax.random.randint(jax.random.fold_in(key, 22), (), 0, block_count)
    counts = jnp.where(jnp.arange(block_count) == forced, TMAX, counts)
    block_keys = jax.random.split(jax.random.fold_in(key, 23), block_count)
    orders = jax.vmap(lambda block_key: jax.random.permutation(block_key, HEADS_DEV))(block_keys)
    return (orders < counts[:, None]).astype(jnp.int32).reshape(HEADS)


def draw_tile_neighbours(key, part):
    window = TILES_DEV + 2 * FACE
    tile_ids = jnp.arange(TILES, dtype=jnp.int32)
    partition = tile_ids // TILES_DEV
    within = tile_ids % TILES_DEV
    candidates = jnp.arange(window, dtype=jnp.int32)
    global_ids = partition[:, None] * TILES_DEV - FACE + candidates[None, :]
    usable = (global_ids >= 0) & (global_ids < TILES) & (candidates[None, :] != FACE + within[:, None])
    tile_keys = jax.random.split(jax.random.fold_in(key, 31), TILES)
    ranks = jax.vmap(lambda tile_key: jax.random.permutation(tile_key, window))(tile_keys).astype(jnp.int32)
    ranks = jnp.where(usable, ranks, -1)
    unused, picked = lax.top_k(ranks, NBR)
    return jnp.take_along_axis(global_ids, picked, axis=1).astype(jnp.int32)


def with_ends(values, key, least, largest):
    longest = values.shape.index(max(values.shape))
    spots = []
    for shift in (0, 1):
        where = [jax.random.randint(jax.random.fold_in(key, axis), (), 0, length) for axis, length in enumerate(values.shape)]
        where[longest] = (where[longest] + shift) % values.shape[longest]
        spots.append(tuple(where))
    return values.at[spots[0]].set(least).at[spots[1]].set(largest)


def block_levels(own_key, dims, cuts, low, largest):
    level = 1.0
    for dim, shards_of in cuts:
        heights = jax.random.uniform(jax.random.fold_in(jax.random.fold_in(own_key, 6), dim), (shards_of,), jnp.float32, low / len(cuts), largest / len(cuts))
        level = level * jnp.repeat(jnp.exp(heights), dims[dim] // shards_of).reshape((-1,) + (1,) * (len(dims) - 1 - dim))
    return level


def scatter_about(key, extent, scale, most, cuts=(), kind=jnp.bfloat16):
    entries = jax.random.normal(key, extent, jnp.float32) * scale
    if len(cuts) > 0:
        entries = block_levels(key, extent, cuts, -0.22, 0.18) * entries
    return jnp.clip(entries, min=-most, max=most).astype(kind)


def setup_inputs(seed: int = 0) -> dict:
    key_list = jax.random.split(jax.random.key(seed), 7)
    return {
        "queries": draw_queries(jax.random.fold_in(key_list[6], 71), 0),
        "keys_values": draw_keys_values(jax.random.fold_in(key_list[6], 71), 0),
        "head_kind": draw_head_kind(jax.random.fold_in(key_list[6], 71), 0),
        "tile_neighbours": draw_tile_neighbours(jax.random.fold_in(key_list[6], 71), 0),
        "tile_mask": with_ends((jax.random.randint(key_list[4], (TILES, NBR), 0, 3) < 2).astype(jnp.int32), jax.random.fold_in(key_list[4], 1), 0, 1),
        "out_weight": scatter_about(key_list[5], (HEADS * HD, D), (HEADS * HD) ** -0.5, 0.078125, ((0, 4),)),
    }


def reference(queries, keys_values, head_kind, tile_neighbours, tile_mask, out_weight):
    score_scale = HD ** -0.5
    query_heads = jnp.transpose(queries, (1, 0, 2))
    key_heads = jnp.transpose(keys_values[0], (1, 0, 2))
    value_heads = jnp.transpose(keys_values[1], (1, 0, 2))
    own_tiles = jnp.arange(TILES, dtype=jnp.int32)
    key_tiles = jnp.concatenate([own_tiles[:, None], tile_neighbours.astype(jnp.int32)], axis=1)
    allowed_tiles = jnp.concatenate([jnp.ones((TILES, 1), dtype=bool), tile_mask == 1], axis=1)
    allowed_keys = jnp.repeat(allowed_tiles, TILE, axis=1)

    def global_head(query_rows, key_rows, value_rows):
        blocks = query_rows.reshape(TOKENS // TOK_DEV, TOK_DEV, HD)

        def one_block(block_rows):
            scores = jnp.dot(block_rows, key_rows.T, preferred_element_type=jnp.float32) * score_scale
            top_score = jnp.max(scores, axis=1, keepdims=True)
            exponent = jnp.exp(scores - top_score)
            weight_sum = jnp.sum(exponent, axis=1, keepdims=True)
            mixed = jnp.dot(exponent.astype(jnp.bfloat16), value_rows, preferred_element_type=jnp.float32)
            return mixed / weight_sum

        return lax.map(one_block, blocks).reshape(TOKENS, HD)

    def tile_head(query_rows, key_rows, value_rows):
        query_tiles = query_rows.reshape(TILES, TILE, HD).astype(jnp.float32)
        key_sets = key_rows.reshape(TILES, TILE, HD)[key_tiles].reshape(TILES, (NBR + 1) * TILE, HD)
        value_sets = value_rows.reshape(TILES, TILE, HD)[key_tiles].reshape(TILES, (NBR + 1) * TILE, HD)
        scores = jnp.einsum("tqd,tkd->tqk", query_tiles, key_sets.astype(jnp.float32)) * score_scale
        scores = jnp.where(allowed_keys[:, None, :], scores, -1e30)
        top_score = jnp.max(scores, axis=2, keepdims=True)
        exponent = jnp.where(allowed_keys[:, None, :], jnp.exp(scores - top_score), 0.0)
        weight_sum = jnp.sum(exponent, axis=2, keepdims=True)
        rounded = exponent.astype(jnp.bfloat16).astype(jnp.float32)
        mixed = jnp.einsum("tqk,tkd->tqd", rounded, value_sets.astype(jnp.float32))
        return (mixed / weight_sum).reshape(TOKENS, HD)

    def one_head(operands):
        kind_value, query_rows, key_rows, value_rows = operands
        result = lax.cond(kind_value == 1, global_head, tile_head, query_rows, key_rows, value_rows)
        return result.astype(jnp.bfloat16)

    attention = lax.map(one_head, (head_kind, query_heads, key_heads, value_heads))
    weight_heads = out_weight.reshape(HEADS, HD, D)
    projected = jnp.zeros((TOKENS, D), jnp.float32)
    for block_index in range(HEADS // HEADS_DEV):
        first_head = block_index * HEADS_DEV
        partial_sum = jnp.einsum("htd,hde->te", attention[first_head:first_head + HEADS_DEV].astype(jnp.float32), weight_heads[first_head:first_head + HEADS_DEV].astype(jnp.float32))
        projected = projected + partial_sum.astype(jnp.bfloat16).astype(jnp.float32)
    return projected.astype(jnp.bfloat16)
```

```python
import functools

import jax
import jax.numpy as jnp
from jax import lax
from jax.experimental import pallas as pl
from jax.experimental.pallas import tpu as pltpu
from jax.sharding import PartitionSpec as P

FACE = 1
LOG2E = 1.4426950408889634


def temporal_slots(heads_local):
    return max(1, (heads_local * 2) // 5)


def pack_kernel(slots, tile_rows, order, kv_ref, k_out, v_out, tail_out, head_out, sems):
    heads = kv_ref.shape[1]
    tok_rows = kv_ref.shape[2]
    rest = heads - slots
    copies = []
    for part, out in ((0, k_out), (1, v_out)):
        for s in range(slots):
            copies.append((kv_ref.at[part, order[s]], out.at[s]))
    for part in range(2):
        for r in range(rest):
            source = kv_ref.at[part, order[slots + r]]
            copies.append((source.at[pl.ds(tok_rows - tile_rows, tile_rows)], tail_out.at[part, r]))
            copies.append((source.at[pl.ds(0, tile_rows)], head_out.at[part, r]))
    started = []
    for i, (source, target) in enumerate(copies):
        copy = pltpu.make_async_copy(source, target, sems.at[i])
        copy.start()
        started.append(copy)
    for copy in started:
        copy.wait()


def pack_heads(order, kv_heads, slots, tile_rows):
    _, heads, tok_rows, width = kv_heads.shape
    rest = heads - slots
    dtype = kv_heads.dtype
    any_spec = pl.BlockSpec(memory_space=pl.ANY)
    return pl.pallas_call(
        functools.partial(pack_kernel, slots, tile_rows),
        out_shape=(
            jax.ShapeDtypeStruct((slots, tok_rows, width), dtype),
            jax.ShapeDtypeStruct((slots, tok_rows, width), dtype),
            jax.ShapeDtypeStruct((2, rest, FACE * tile_rows, width), dtype),
            jax.ShapeDtypeStruct((2, rest, FACE * tile_rows, width), dtype),
        ),
        grid_spec=pltpu.PrefetchScalarGridSpec(
            num_scalar_prefetch=1,
            grid=(1,),
            in_specs=[any_spec],
            out_specs=(any_spec,) * 4,
            scratch_shapes=[pltpu.SemaphoreType.DMA((2 * slots + 4 * rest,))],
        ),
        name="pack",
    )(order, kv_heads)


def with_ones(values):
    return jnp.concatenate([values, jnp.ones_like(values)], axis=1)


def scaled_scores(queries, keys):
    factor = (queries.shape[1] ** -0.5) * LOG2E
    return (
        lax.dot_general(queries, keys, (((1,), (1,)), ((), ())), preferred_element_type=jnp.float32)
        * factor
    )


def sliding_kernel(order, window_ids, mask, q_ref, k_ref, v_ref, before_ref, after_ref, out_ref, keys, values):
    tile_rows = before_ref.shape[2]
    tok_rows, width = q_ref.shape[1], q_ref.shape[2]
    listed = mask.shape[1]
    keys[0:tile_rows] = before_ref[0, 0]
    keys[tile_rows : tile_rows + tok_rows] = k_ref[0, 0]
    keys[tile_rows + tok_rows :] = after_ref[0, 0]
    values[0:tile_rows, 0:width] = before_ref[1, 0]
    values[tile_rows : tile_rows + tok_rows, 0:width] = v_ref[0, 0]
    values[tile_rows + tok_rows :, 0:width] = after_ref[1, 0]

    @pl.when(pl.program_id(0) == 0)
    def _():
        values[:, width:] = jnp.ones_like(values[:, width:])

    for tile in range(tok_rows // tile_rows):
        queries = q_ref[0, tile * tile_rows : (tile + 1) * tile_rows]
        starts = [(FACE + tile) * tile_rows]
        for n in range(listed):
            starts.append(pl.multiple_of(window_ids[tile, n] * tile_rows, tile_rows))
        scores = []
        for n, start in enumerate(starts):
            block = scaled_scores(queries, keys[pl.ds(start, tile_rows), :])
            if n > 0:
                block = jnp.where(mask[tile, n - 1] == 1, block, -jnp.inf)
            scores.append(block)
        top = scores[0].max(axis=1, keepdims=True)
        for block in scores[1:]:
            top = jnp.maximum(top, block.max(axis=1, keepdims=True))
        total = None
        for block, start in zip(scores, starts):
            weights = jnp.exp2(block - top).astype(jnp.bfloat16)
            mixed = jnp.dot(
                weights, values[pl.ds(start, tile_rows), :], preferred_element_type=jnp.float32
            )
            total = mixed if total is None else total + mixed
        out_ref[tile * tile_rows : (tile + 1) * tile_rows, :] = (
            total[:, :width] / total[:, width:]
        ).astype(out_ref.dtype)


def sliding_heads(order, window_ids, mask, q_heads, kv_heads, before, after, slots):
    heads, tok_rows, width = q_heads.shape
    rest = heads - slots
    tile_rows = before.shape[2] // FACE
    window_rows = tok_rows + 2 * FACE * tile_rows
    return pl.pallas_call(
        sliding_kernel,
        out_shape=jax.ShapeDtypeStruct((tok_rows, heads * width), q_heads.dtype),
        grid_spec=pltpu.PrefetchScalarGridSpec(
            num_scalar_prefetch=3,
            grid=(rest,),
            in_specs=[
                pl.BlockSpec((1, tok_rows, width), lambda i, o, w, m: (o[slots + i], 0, 0)),
                pl.BlockSpec((1, 1, tok_rows, width), lambda i, o, w, m: (0, o[slots + i], 0, 0)),
                pl.BlockSpec((1, 1, tok_rows, width), lambda i, o, w, m: (1, o[slots + i], 0, 0)),
                pl.BlockSpec((2, 1, FACE * tile_rows, width), lambda i, o, w, m: (0, i, 0, 0)),
                pl.BlockSpec((2, 1, FACE * tile_rows, width), lambda i, o, w, m: (0, i, 0, 0)),
            ],
            out_specs=pl.BlockSpec((tok_rows, width), lambda i, o, w, m: (0, o[slots + i])),
            scratch_shapes=[
                pltpu.VMEM((window_rows, width), q_heads.dtype),
                pltpu.VMEM((window_rows, 2 * width), q_heads.dtype),
            ],
        ),
        name="sliding",
    )(order, window_ids, mask, q_heads, kv_heads, kv_heads, before, after)


def online_block(q_ref, keys, values, total, top, rows):
    scores = scaled_scores(q_ref[0, rows], keys)
    old_top = top[rows]
    new_top = jnp.maximum(old_top, scores.max(axis=1, keepdims=True))
    factor = jnp.exp2(old_top - new_top)
    weights = jnp.exp2(scores - new_top[:, :1]).astype(jnp.bfloat16)
    mixed = jnp.dot(weights, values, preferred_element_type=jnp.float32)
    total[rows] = total[rows] * jnp.concatenate([factor, factor], axis=1) + mixed
    top[rows] = new_top


def temporal_kernel(
    chunk_count, tiles, query_rows, first, last, order, count, allowed, q_ref, *refs
):
    chunks = refs[: 2 * chunk_count]
    refs = refs[2 * chunk_count :]
    if not first:
        total_in, top_in = refs[:2]
        refs = refs[2:]
    if last:
        refs = refs[1:]
        out_ref, total, top = refs
    else:
        total_ref, top_ref = refs
        total, top = total_ref.at[0], top_ref.at[0]
    slot = pl.program_id(0)
    tok_rows, width = q_ref.shape[1], q_ref.shape[2]
    tile_rows = tok_rows // tiles
    if first:
        total[...] = jnp.zeros_like(total)
        top[...] = jnp.full_like(top, -jnp.inf)
    else:
        total[...] = total_in[0]
        top[...] = top_in[0]

    @pl.when(slot < count[0])
    def _():
        for c in range(chunk_count):
            values = with_ones(chunks[2 * c + 1][0])
            for start in range(0, tok_rows, query_rows):
                online_block(
                    q_ref, chunks[2 * c][0], values, total, top, slice(start, start + query_rows)
                )

    @pl.when(slot >= count[0])
    def _():
        for c in range(chunk_count):
            for key_tile in range(tiles):
                for tile in range(tiles):

                    @pl.when(allowed[c, key_tile * tiles + tile] == 1)
                    def _():
                        span = slice(key_tile * tile_rows, (key_tile + 1) * tile_rows)
                        online_block(
                            q_ref,
                            chunks[2 * c][0, span],
                            with_ones(chunks[2 * c + 1][0, span]),
                            total,
                            top,
                            slice(tile * tile_rows, (tile + 1) * tile_rows),
                        )

    if last:
        out_ref[...] = (total[:, :width] / total[:, width:]).astype(out_ref.dtype)


def temporal_heads(order, count, allowed, q_heads, chunks, state, attention, tiles):
    heads, tok_rows, width = q_heads.shape
    slots = chunks[0][0].shape[0]
    first, last = state is None, attention is not None
    query_rows = tok_rows // 2
    head_spec = pl.BlockSpec((1, tok_rows, width), lambda s, o, n, a: (s, 0, 0))
    total_spec = pl.BlockSpec((1, tok_rows, 2 * width), lambda s, o, n, a: (s, 0, 0))
    operands = [q_heads]
    in_specs = [pl.BlockSpec((1, tok_rows, width), lambda s, o, n, a: (o[s], 0, 0))]
    for keys, values in chunks:
        operands += [keys, values]
        in_specs += [head_spec, head_spec]
    if not first:
        operands += list(state)
        in_specs += [total_spec, head_spec]
    aliases = {}
    scratch = []
    if last:
        aliases = {3 + len(operands): 0}
        operands.append(attention)
        in_specs.append(pl.BlockSpec(memory_space=pl.ANY))
        out_shape = jax.ShapeDtypeStruct(attention.shape, attention.dtype)
        out_specs = pl.BlockSpec((tok_rows, width), lambda s, o, n, a: (0, o[s]))
        scratch = [
            pltpu.VMEM((tok_rows, 2 * width), jnp.float32),
            pltpu.VMEM((tok_rows, width), jnp.float32),
        ]
    else:
        out_shape = (
            jax.ShapeDtypeStruct((slots, tok_rows, 2 * width), jnp.float32),
            jax.ShapeDtypeStruct((slots, tok_rows, width), jnp.float32),
        )
        out_specs = (total_spec, head_spec)
    return pl.pallas_call(
        functools.partial(temporal_kernel, len(chunks), tiles, query_rows, first, last),
        out_shape=out_shape,
        grid_spec=pltpu.PrefetchScalarGridSpec(
            num_scalar_prefetch=3,
            grid=(slots,),
            in_specs=in_specs,
            out_specs=out_specs,
            scratch_shapes=scratch,
        ),
        input_output_aliases=aliases,
        name="temporal",
    )(order, count, allowed, *operands)


def gather_chunks(keys, values):
    count = lax.axis_size("frame")

    def swap(cells, bit):
        return lax.ppermute(cells, "frame", [(i, i ^ bit) for i in range(count)])

    chunks = {0: (keys, values)}
    for offset in sorted(range(1, count), key=lambda e: (bin(e >> 1).count("1"), e)):
        high = offset & ~1
        if offset & 1:
            source = chunks[offset ^ 1]
            chunks[offset] = (swap(source[0], 1), swap(source[1], 1))
            continue
        low_bit = high & -high
        top_bit = 1 << (high.bit_length() - 1)
        if low_bit == top_bit:
            chunks[offset] = (swap(keys, offset), swap(values, offset))
        else:
            chunks[offset] = (
                swap(chunks[offset ^ low_bit][0], low_bit),
                swap(chunks[offset ^ top_bit][1], top_bit),
            )
    return chunks


def sum_over_head(project):
    me = lax.axis_index("head")
    halves = (0, 1)
    right = [(0, 1), (1, 2), (2, 3)]
    left = [(3, 2), (2, 1), (1, 0)]

    def shift(cells, pairs):
        return lax.ppermute(cells, "head", pairs)

    first = [shift(project(3 - me, c, ()), [right[0], left[0]]) for c in halves]
    second = [project((me + 2) % 4, c, (first[c],)) for c in halves]
    second = [(shift(x, right[:2]), shift(x, left[:2])) for x in second]
    third = []
    for c in halves:
        to_right = project(jnp.minimum(me + 1, 3), c, (second[c][0],))
        to_left = project(jnp.maximum(me - 1, 0), c, (second[c][1],))
        third.append((shift(to_right, right), shift(to_left, left)))
    return jnp.concatenate([project(me, c, third[c]) for c in halves], axis=1)


def per_device(queries, keys_values, head_kind, tile_neighbours, tile_mask, out_weight):
    tok_rows, heads_local, head_width = queries.shape
    tiles_local = tile_neighbours.shape[0]
    tile_rows = tok_rows // tiles_local
    slots = temporal_slots(heads_local)
    frames = lax.axis_size("frame")
    partition = lax.axis_index("frame")

    q_heads = jnp.transpose(queries, (1, 0, 2))
    kv_heads = jnp.transpose(keys_values, (0, 2, 1, 3))

    temporal = (head_kind == 1).astype(jnp.int32)
    ids = jnp.arange(heads_local, dtype=jnp.int32)
    earlier = ids[None, :] < ids[:, None]
    count = jnp.sum(temporal)
    rank = jnp.where(
        temporal == 1,
        jnp.sum(jnp.where(earlier, temporal[None, :], 0), axis=1),
        count + jnp.sum(jnp.where(earlier, 1 - temporal[None, :], 0), axis=1),
    )
    order = jnp.sum(jnp.where(rank[None, :] == ids[:, None], ids[None, :], 0), axis=1)

    own_tiles = partition * tiles_local + jnp.arange(tiles_local, dtype=jnp.int32)
    window_ids = jnp.clip(
        tile_neighbours - (partition * tiles_local - FACE), 0, tiles_local + 2 * FACE - 1
    )
    offsets = jnp.arange(frames, dtype=jnp.int32)
    chunk_tiles = (partition ^ offsets)[:, None] * tiles_local + jnp.arange(
        tiles_local, dtype=jnp.int32
    )
    named = (tile_neighbours[None, None, :, :] == chunk_tiles[:, :, None, None]) & (
        tile_mask[None, None, :, :] == 1
    )
    allowed = (
        jnp.any(named, axis=3) | (chunk_tiles[:, :, None] == own_tiles[None, None, :])
    ).astype(jnp.int32)
    allowed = allowed.reshape(frames, tiles_local * tiles_local)

    keys, values, tail, head = pack_heads(order, kv_heads, slots, tile_rows)
    before = lax.ppermute(tail, "frame", [(i, i + 1) for i in range(frames - 1)])
    after = lax.ppermute(head, "frame", [(i + 1, i) for i in range(frames - 1)])
    chunks = gather_chunks(keys, values)

    attention = sliding_heads(
        order, window_ids, tile_mask, q_heads, kv_heads, before, after, slots
    )
    groups = [[0, 1], [e for e in range(2, frames) if bin(e >> 1).count("1") == 1]]
    groups.append([e for e in range(frames) if e not in groups[0] + groups[1]])
    state = None
    for number, group in enumerate(groups):
        state = temporal_heads(
            order,
            count[None],
            jnp.stack([allowed[e] for e in group]),
            q_heads,
            [chunks[e] for e in group],
            state,
            attention if number == len(groups) - 1 else None,
            tiles_local,
        )
    attention = state

    blocks = lax.axis_size("head")
    if blocks != 4:
        return lax.psum_scatter(
            jnp.dot(attention, out_weight, preferred_element_type=jnp.float32).astype(jnp.bfloat16),
            "head",
            scatter_dimension=0,
            tiled=True,
        )
    block_rows = tok_rows // blocks
    half = out_weight.shape[1] // 2

    def project(block, column_half, addends):
        rows = lax.dynamic_slice_in_dim(attention, block * block_rows, block_rows, 0)
        columns = lax.slice_in_dim(out_weight, column_half * half, (column_half + 1) * half, axis=1)
        share = jnp.dot(rows, columns, preferred_element_type=jnp.float32)
        for addend in addends:
            share = share + addend.astype(jnp.float32)
        return share.astype(jnp.bfloat16)

    return sum_over_head(project)


def solution(mesh):
    return jax.shard_map(
        per_device,
        mesh=mesh,
        in_specs=(
            P("frame", "head", None),
            P(None, "frame", "head", None),
            P("head"),
            P("frame", None),
            P("frame", None),
            P("head", None),
        ),
        out_specs=P(("frame", "head"), None),
        check_vma=False,
    )
```
